32 devices in a mesh: sector: 4 (over y, x), shard: 8 (over z, core).
Axes of the slice: x: 2, y: 2, z: 4, core: 2. Of those that a mesh axis runs over, the one named last changes fastest.
Arguments:
- wavefunction: bfloat16 [4, 768, 12288], P('sector', None, 'shard'), may hold values from -6 to 6
- left_environment: bfloat16 [2, 4, 768, 768], P(None, 'sector', 'shard'), may hold values from -0.21875 to 0.21875
- right_environment: bfloat16 [2, 4, 768, 768], P(None, 'sector', 'shard'), may hold values from -0.21875 to 0.21875
- targets: int32 [2, 4], replicated, may hold values from 0 to 3
- bond_sizes: int32 [2, 4], replicated, may hold values from 384 to 768, as said below
Outputs:
- applied: bfloat16 [4, 768, 12288], P('sector', 'shard')
The draws below stay inside these ranges and needn't reach their ends.
Inputs may be any that keep to these rules, and one draw needn't show every extreme that they name: `bond_sizes`: each of the two rows reaches 768 at some block.
All inputs are finite; a program needn't handle non-finite values.
Results may differ from the reference program's by a relative error of at most 0.0055.
Values may be sent and summed in bfloat16 or wider, within the bound.
No kernel may reach another device: no remote copies, remote signals or barrier semaphores. Data moves between devices by JAX's collectives and lax.ppermute only.
A program may use at most 64 MiB of HBM per device.

```python
import jax
import jax.numpy as jnp
from jax import lax

BOND = 768
PHYS = 16
CHANNELS = 2
BLOCKS = 4


def draw_bond_sizes(key, part):
    first, second = jax.random.split(jax.random.fold_in(key, 11))
    sizes = jax.random.randint(first, (2, BLOCKS), BOND // 2, BOND + 1)
    largest = jax.random.randint(second, (2,), 0, BLOCKS)
    at_largest = jnp.arange(BLOCKS)[None, :] == largest[:, None]
    return jnp.where(at_largest, BOND, sizes).astype(jnp.int32)


def touch_ends(entries, own_key, smallest, high):
    place = [jax.random.randint(jax.random.fold_in(own_key, axis), (), 0, length) for axis, length in enumerate(entries.shape)]
    main_axis = entries.shape.index(max(entries.shape))
    neighbour = place[:main_axis] + [(place[main_axis] + 1) % entries.shape[main_axis]] + place[main_axis + 1:]
    return entries.at[tuple(place)].set(smallest).at[tuple(neighbour)].set(high)


def levels(stream_key, dims, cuts, smallest, high):
    gain = 1.0
    for axis_at, parts in cuts:
        draws = jax.random.uniform(jax.random.fold_in(jax.random.fold_in(stream_key, 6), axis_at), (parts,), jnp.float32, smallest / len(cuts), high / len(cuts))
        gain = gain * jnp.repeat(jnp.exp(draws), dims[axis_at] // parts).reshape((-1,) + (1,) * (len(dims) - 1 - axis_at))
    return gain


def noise(rng, extent, spread, most, cuts=(), held_as=jnp.bfloat16):
    array = jax.random.normal(rng, extent, jnp.float32) * spread
    if len(cuts) > 0:
        array = levels(rng, extent, cuts, -0.22, 0.18) * array
    return jnp.clip(array, min=-most, max=most).astype(held_as)


def setup_inputs(seed: int = 0) -> dict:
    key_of = jax.random.split(jax.random.key(seed), 6)
    return {
        "wavefunction": noise(key_of[0], (BLOCKS, BOND, PHYS * BOND), 1.0, 6.0, ((0, 4), (2, 8))),
        "left_environment": noise(key_of[1], (CHANNELS, BLOCKS, BOND, BOND), BOND ** -0.5, 0.21875, ((1, 4), (2, 8))),
        "right_environment": noise(key_of[2], (CHANNELS, BLOCKS, BOND, BOND), BOND ** -0.5, 0.21875, ((1, 4), (2, 8))),
        "targets": touch_ends(jax.random.randint(key_of[3], (CHANNELS, BLOCKS), 0, BLOCKS), jax.random.fold_in(key_of[3], 1), 0, BLOCKS - 1).astype(jnp.int32),
        "bond_sizes": draw_bond_sizes(jax.random.fold_in(key_of[5], 71), 0),
    }


def reference(wavefunction, left_environment, right_environment, targets, bond_sizes):
    positions = jnp.arange(BOND, dtype=jnp.int32)
    left_mask = positions[None, :] < bond_sizes[0][:, None]
    right_mask = positions[None, :] < bond_sizes[1][:, None]
    column_mask = jnp.tile(right_mask, (1, PHYS))
    psi_live = jnp.where(left_mask[:, :, None] & column_mask[:, None, :], wavefunction, jnp.zeros_like(wavefunction))
    accumulated = jnp.zeros((BLOCKS, BOND, PHYS * BOND), jnp.float32)
    for channel in range(CHANNELS):
        destination = targets[channel]

        def left_product(operands):
            environment_block, state_block, row_live, col_live = operands
            env_live = jnp.where(row_live[:, None] & col_live[None, :], environment_block, jnp.zeros_like(environment_block))
            return jnp.dot(env_live, state_block, preferred_element_type=jnp.float32).astype(jnp.bfloat16)

        halves = lax.map(left_product, (left_environment[channel], psi_live, left_mask[destination], left_mask))
        arrived = jax.ops.segment_sum(halves.astype(jnp.float32), destination, num_segments=BLOCKS).astype(jnp.bfloat16)

        def right_product(operands):
            arrived_block, environment_block, live_mask = operands
            env_live = jnp.where(live_mask[:, None] & live_mask[None, :], environment_block, jnp.zeros_like(environment_block))
            flat_rows = arrived_block.reshape(BOND * PHYS, BOND)
            product = lax.dot_general(flat_rows, env_live, (((1,), (1,)), ((), ())), preferred_element_type=jnp.float32)
            return product.reshape(BOND, PHYS * BOND)

        accumulated = accumulated + lax.map(right_product, (arrived, right_environment[channel], right_mask))
    return accumulated.astype(jnp.bfloat16)
```

```python
import math

import jax
import jax.numpy as jnp
from jax import lax
from jax.sharding import PartitionSpec as P


def is_pow2(n):
    return n & (n - 1) == 0


def exchange(x, axis, offset):
    size = lax.axis_size(axis)
    return lax.ppermute(x, axis, [(a, a ^ offset) for a in range(size)])


def gather_pieces(piece):
    size = lax.axis_size("shard")
    near = [piece] + [exchange(piece, "shard", m) for m in range(2, size, 2)]
    near = jnp.stack(near)
    return jnp.concatenate([near, exchange(near, "shard", 1)])


def piece_order(size):
    return list(range(0, size, 2)) + list(range(1, size, 2))


def fast(wavefunction, left_environment, right_environment, targets, bond_sizes):
    sector = lax.axis_index("sector")
    shard = lax.axis_index("shard")
    blocks = lax.axis_size("sector")
    shards_n = lax.axis_size("shard")
    channels, _, rows, bond = left_environment.shape
    phys = wavefunction.shape[2] // bond
    col_parts = math.gcd(blocks, phys)
    row_parts = blocks // col_parts
    sub = rows // row_parts
    wide = (phys // col_parts) * bond
    order = piece_order(shards_n)
    left_live, right_live = bond_sizes[0], bond_sizes[1]
    own_row, own_col = sector // col_parts, sector % col_parts
    positions = jnp.arange(bond, dtype=jnp.int32)
    own_positions = shard * rows + jnp.arange(rows, dtype=jnp.int32)

    f_own = right_environment[:, 0]
    f_parts = [f_own] + [exchange(f_own, "sector", k) for k in range(1, blocks)]
    e_all, f_all = [], []
    for c in range(channels):
        target = targets[c, sector]
        keep = (own_positions < left_live[target])[:, None] & (positions < left_live[sector])[None, :]
        e = jnp.where(keep, left_environment[c, 0], 0).reshape(row_parts, sub, bond)
        e = jnp.stack([lax.dynamic_index_in_dim(e, own_row ^ k, 0, False) for k in range(row_parts)])
        e_all.append(gather_pieces(e))
        f = f_parts[0][c]
        for k in range(1, blocks):
            f = jnp.where(target == sector ^ k, f_parts[k][c], f)
        live = jnp.minimum(right_live[target], right_live[sector])
        keep = (own_positions < right_live[target])[:, None] & (positions < live)[None, :]
        f_rel = gather_pieces(jnp.where(keep, f, 0))
        place = jnp.array([order.index(m) for m in range(shards_n)], jnp.int32)
        f_abs = jnp.take(f_rel, place[shard ^ jnp.arange(shards_n)], axis=0)
        f_all.append(f_abs.reshape(bond, bond))

    psi = wavefunction[0]
    psi_parts = [lax.dynamic_slice_in_dim(psi, (own_col ^ k) * wide, wide, 1) for k in range(col_parts)]
    rows_all = shards_n * sub
    received = [[None] * blocks for _ in range(channels)]
    for c in range(channels):
        for k in list(range(1, blocks)) + [0]:
            left = e_all[c][:, k // col_parts].reshape(rows_all, bond)
            half = jnp.dot(left, psi_parts[k % col_parts], preferred_element_type=jnp.float32).astype(jnp.bfloat16)
            half = half.reshape(rows_all, phys // col_parts, bond)
            y = jnp.concatenate([
                lax.dot_general(half[:, p], f_all[c], (((1,), (1,)), ((), ())), preferred_element_type=jnp.float32)
                .astype(jnp.bfloat16) for p in range(phys // col_parts)], axis=1)
            received[c][k] = exchange(y, "sector", k) if k else y

    out = jnp.zeros((rows, shards_n * phys * bond), jnp.bfloat16)
    for j in range(blocks):
        total = jnp.zeros((rows_all, wide), jnp.float32)
        for c in range(channels):
            for k in range(blocks):
                hit = targets[c, sector ^ k] == sector ^ j
                total = total + jnp.where(hit, received[c][k], 0).astype(jnp.float32)
        total = total.astype(jnp.bfloat16)
        if j:
            total = exchange(total, "sector", j)
        total = total.reshape(shards_n, sub, wide)
        row_at = (own_row ^ (j // col_parts)) * sub
        col_at = (own_col ^ (j % col_parts)) * wide
        for n, m in enumerate(order):
            part = exchange(total[n], "shard", m) if m else total[n]
            out = lax.dynamic_update_slice(out, part, (row_at, (shard ^ m) * phys * bond + col_at))
    return out[None]


def shards(wavefunction, left_environment, right_environment, targets, bond_sizes):
    group_index = lax.axis_index("sector")
    shard_index = lax.axis_index("shard")
    blocks = lax.axis_size("sector")
    channels = left_environment.shape[0]
    bond_dim = left_environment.shape[3]
    col_width = wavefunction.shape[2]
    positions = jnp.arange(bond_dim, dtype=jnp.int32)
    left_live = bond_sizes[0]
    right_live = bond_sizes[1]
    own_left = positions < left_live[group_index]
    own_right = positions < right_live[group_index]
    columns = shard_index * col_width + jnp.arange(col_width, dtype=jnp.int32)
    column_live = columns % bond_dim < right_live[group_index]
    psi_live = jnp.where(
        own_left[:, None] & column_live[None, :], wavefunction[0], jnp.zeros_like(wavefunction[0])
    )
    destination = targets[:, group_index]
    target_live = left_live[destination]
    env_rows = lax.all_gather(left_environment[:, 0], "shard", axis=1, tiled=True)
    row_ids = jnp.arange(env_rows.shape[1], dtype=jnp.int32)
    keep_mask = (row_ids[None, :, None] < target_live[:, None, None]) & own_left[None, None, :]
    env_live = jnp.where(keep_mask, env_rows, jnp.zeros_like(env_rows))
    halves = jnp.einsum(
        "crk,kw->crw", env_live, psi_live, preferred_element_type=jnp.float32
    ).astype(jnp.bfloat16)
    sector_ids = jnp.arange(blocks, dtype=jnp.int32)
    assign = (targets[:, None, :] == sector_ids[None, :, None]).astype(jnp.bfloat16)
    row_slabs = halves.reshape(channels, blocks, bond_dim // blocks, col_width)
    received = lax.all_to_all(row_slabs, "sector", split_axis=1, concat_axis=1, tiled=True)
    summed = jnp.einsum(
        "ctq,cqrw->ctrw", assign, received, preferred_element_type=jnp.float32
    ).astype(jnp.bfloat16)
    returned = lax.all_to_all(summed, "sector", split_axis=1, concat_axis=1, tiled=True)
    gathered_cols = returned.reshape(channels, bond_dim, col_width)
    arrived = lax.all_to_all(gathered_cols, "shard", split_axis=1, concat_axis=2, tiled=True)
    local_rows = arrived.shape[1]
    phys_count = arrived.shape[2] // bond_dim
    stacked = arrived.reshape(channels, local_rows, phys_count, bond_dim)
    env_rows = lax.all_gather(right_environment[:, 0], "shard", axis=1, tiled=True)
    row_ids = jnp.arange(env_rows.shape[1], dtype=jnp.int32)
    keep_mask = (row_ids < right_live[group_index])[None, :, None] & own_right[None, None, :]
    env_live = jnp.where(keep_mask, env_rows, jnp.zeros_like(env_rows))
    result = jnp.einsum("crpk,cnk->rpn", stacked, env_live, preferred_element_type=jnp.float32)
    return result.reshape(1, local_rows, phys_count * bond_dim).astype(jnp.bfloat16)


def fits(mesh, shape):
    blocks, shards_n = mesh.shape["sector"], mesh.shape["shard"]
    bond = shape[1]
    local = shape[2] // shards_n
    if local % bond or bond % shards_n or not (is_pow2(blocks) and is_pow2(shards_n)) or shards_n < 2:
        return False
    col_parts = math.gcd(blocks, local // bond)
    return (bond // shards_n) % (blocks // col_parts * 16) == 0


def solution(mesh):
    def whole(*arrays):
        body = fast if fits(mesh, arrays[0].shape) else shards
        return jax.shard_map(
            body,
            mesh=mesh,
            in_specs=(
                P("sector", None, "shard"),
                P(None, "sector", "shard", None),
                P(None, "sector", "shard", None),
                P(),
                P(),
            ),
            out_specs=P("sector", "shard", None),
            check_vma=False,
        )(*arrays)

    return whole
```

```python
import functools
import math

import jax
import jax.numpy as jnp
from jax import lax
from jax.experimental import pallas as pl
from jax.experimental.pallas import tpu as pltpu
from jax.sharding import PartitionSpec as P


def is_pow2(n):
    return n & (n - 1) == 0


def exchange(x, axis, offset):
    size = lax.axis_size(axis)
    return lax.ppermute(x, axis, [(a, a ^ offset) for a in range(size)])


def gather_pieces(piece):
    pieces = []
    for m in range(0, lax.axis_size("shard"), 2):
        near = exchange(piece, "shard", m) if m else piece
        pieces += [near, exchange(near, "shard", 1)]
    return pieces


def live_mask(shape, rows_live, cols_live, row_start):
    row = lax.broadcasted_iota(jnp.int32, shape, 0) + row_start
    col = lax.broadcasted_iota(jnp.int32, shape, 1)
    return (row < rows_live) & (col < cols_live)


def mask_left_kernel(targets, sizes, e_ref, *outs):
    sector, shard = lax.axis_index("sector"), lax.axis_index("shard")
    rows, bond = outs[0].shape
    for c, out in enumerate(outs):
        keep = live_mask((rows, bond), sizes[0, targets[c, sector]], sizes[0, sector], shard * rows)
        out[...] = jnp.where(keep, e_ref[c], 0).astype(out.dtype)


def mask_right_kernel(targets, sizes, *refs, blocks, channel):
    sources, out = refs[:blocks], refs[blocks]
    sector, shard = lax.axis_index("sector"), lax.axis_index("shard")
    target = targets[channel, sector]
    live = sizes[1, target]
    keep = live_mask(out.shape, live, jnp.minimum(live, sizes[1, sector]), shard * out.shape[0])
    for k in range(blocks):
        @pl.when(target == sector ^ k)
        def _(k=k):
            out[...] = jnp.where(keep, sources[k][...], 0).astype(out.dtype)


def masked(kernel, outs, targets, sizes, *arrays):
    rows, bond = arrays[0].shape[-2:]
    full, scalars = pl.BlockSpec(memory_space=pltpu.VMEM), pl.BlockSpec(memory_space=pltpu.SMEM)
    return pl.pallas_call(
        kernel,
        out_shape=[jax.ShapeDtypeStruct((rows, bond), jnp.bfloat16)] * outs,
        in_specs=[scalars] * 2 + [full] * len(arrays),
        out_specs=[full] * outs,
    )(targets, sizes, *arrays)


def products_kernel(*refs, shards_n, row_parts, col_parts, phys):
    e_refs, f_refs = refs[:shards_n], refs[shards_n:2 * shards_n]
    psi_ref = refs[2 * shards_n]
    y_refs = refs[2 * shards_n + 1:-2]
    left_ref, right_ref = refs[-2:]
    rows, bond = e_refs[0].shape
    sub = rows // row_parts
    block = shards_n * sub
    sector, shard = lax.axis_index("sector"), lax.axis_index("shard")
    own_row, own_col = sector // col_parts, sector % col_parts
    for m in range(shards_n):
        right_ref[pl.ds(pl.multiple_of((shard ^ m) * rows, 16), rows), :] = f_refs[m][...]
        for h in range(row_parts):
            at = pl.multiple_of((own_row ^ h) * sub, 16)
            left_ref[h * block + m * sub:h * block + (m + 1) * sub, :] = e_refs[m][pl.ds(at, sub), :]
    for g in range(col_parts):
        for p in range(phys):
            at = pl.multiple_of(((own_col ^ g) * phys + p) * bond, 128)
            half = jnp.dot(left_ref[...], psi_ref[:, pl.ds(at, bond)], preferred_element_type=jnp.float32)
            y = lax.dot_general(half.astype(jnp.bfloat16), right_ref[...], (((1,), (1,)), ((), ())),
                                preferred_element_type=jnp.float32).astype(jnp.bfloat16)
            for h in range(row_parts):
                y_refs[h * col_parts + g][:, p * bond:(p + 1) * bond] = y[h * block:(h + 1) * block]


def products(e_pieces, f_pieces, psi, row_parts, col_parts):
    shards_n = len(e_pieces)
    rows, bond = e_pieces[0].shape
    phys = psi.shape[1] // bond // col_parts
    out = jax.ShapeDtypeStruct((shards_n * rows // row_parts, phys * bond), jnp.bfloat16)
    full = pl.BlockSpec(memory_space=pltpu.VMEM)
    return pl.pallas_call(
        functools.partial(products_kernel, shards_n=shards_n, row_parts=row_parts, col_parts=col_parts,
                          phys=phys),
        out_shape=[out] * (row_parts * col_parts),
        in_specs=[full] * (2 * shards_n + 1),
        out_specs=[full] * (row_parts * col_parts),
        scratch_shapes=[pltpu.VMEM((bond, bond), jnp.bfloat16)] * 2,
        name="products",
    )(*e_pieces, *f_pieces, psi)


def sum_kernel(targets, *refs, blocks):
    sources, outs, acc = refs[:-blocks - 1], refs[-blocks - 1:-1], refs[-1]
    sector = lax.axis_index("sector")
    acc[...] = jnp.zeros_like(acc)
    for n, ref in enumerate(sources):
        j = targets[n // blocks, sector ^ (n % blocks)] ^ sector
        acc[j] = acc[j] + ref[...].astype(jnp.float32)
    for j in range(blocks):
        outs[j][...] = acc[j].astype(jnp.bfloat16)


def destination_sums(targets, sources, blocks, steps):
    rows, width = sources[0].shape
    spec = pl.BlockSpec((rows // steps, width), lambda n: (n, 0))
    return pl.pallas_call(
        functools.partial(sum_kernel, blocks=blocks),
        grid=(steps,),
        out_shape=[jax.ShapeDtypeStruct((rows, width), jnp.bfloat16)] * blocks,
        in_specs=[pl.BlockSpec(memory_space=pltpu.SMEM)] + [spec] * len(sources),
        out_specs=[spec] * blocks,
        scratch_shapes=[pltpu.VMEM((blocks, rows // steps, width), jnp.float32)],
        name="destination_sums",
    )(targets, *sources)


def fast(*arrays):
    return apply_blocks(*arrays)


def apply_blocks(wavefunction, left_environment, right_environment, targets, bond_sizes):
    sector = lax.axis_index("sector")
    shard = lax.axis_index("shard")
    blocks = lax.axis_size("sector")
    shards_n = lax.axis_size("shard")
    channels, _, rows, bond = left_environment.shape
    phys = wavefunction.shape[2] // bond
    col_parts = math.gcd(blocks, phys)
    row_parts = blocks // col_parts
    sub = rows // row_parts
    wide = (phys // col_parts) * bond
    own_row, own_col = sector // col_parts, sector % col_parts
    psi = wavefunction[0]

    e_own = masked(mask_left_kernel, channels, targets, bond_sizes, left_environment[:, 0])
    received = []
    for c in range(channels):
        f_own = right_environment[c, 0]
        f_parts = [f_own] + [exchange(f_own, "sector", k) for k in range(1, blocks)]
        kernel = functools.partial(mask_right_kernel, blocks=blocks, channel=c)
        f_masked, = masked(kernel, 1, targets, bond_sizes, *f_parts)
        e_pieces = gather_pieces(e_own[c])
        f_pieces = gather_pieces(f_masked)
        y = products(e_pieces, f_pieces, psi, row_parts, col_parts)
        received += [exchange(y[k], "sector", k) if k else y[k] for k in range(blocks)]

    totals = destination_sums(targets, received, blocks, 4)
    out = jnp.zeros((rows, shards_n * phys * bond), jnp.bfloat16)
    for j in range(blocks):
        total = exchange(totals[j], "sector", j) if j else totals[j]
        total = total.reshape(shards_n, sub, wide)
        row_at = (own_row ^ (j // col_parts)) * sub
        col_at = (own_col ^ (j % col_parts)) * wide
        for m in range(shards_n):
            part = exchange(total[m], "shard", m) if m else total[m]
            out = lax.dynamic_update_slice(out, part, (row_at, (shard ^ m) * phys * bond + col_at))
    return out[None]


def shards(wavefunction, left_environment, right_environment, targets, bond_sizes):
    group_index = lax.axis_index("sector")
    shard_index = lax.axis_index("shard")
    blocks = lax.axis_size("sector")
    channels = left_environment.shape[0]
    bond_dim = left_environment.shape[3]
    col_width = wavefunction.shape[2]
    positions = jnp.arange(bond_dim, dtype=jnp.int32)
    left_live = bond_sizes[0]
    right_live = bond_sizes[1]
    own_left = positions < left_live[group_index]
    own_right = positions < right_live[group_index]
    columns = shard_index * col_width + jnp.arange(col_width, dtype=jnp.int32)
    column_live = columns % bond_dim < right_live[group_index]
    psi_live = jnp.where(
        own_left[:, None] & column_live[None, :], wavefunction[0], jnp.zeros_like(wavefunction[0])
    )
    destination = targets[:, group_index]
    target_live = left_live[destination]
    env_rows = lax.all_gather(left_environment[:, 0], "shard", axis=1, tiled=True)
    row_ids = jnp.arange(env_rows.shape[1], dtype=jnp.int32)
    keep_mask = (row_ids[None, :, None] < target_live[:, None, None]) & own_left[None, None, :]
    env_live = jnp.where(keep_mask, env_rows, jnp.zeros_like(env_rows))
    halves = jnp.einsum(
        "crk,kw->crw", env_live, psi_live, preferred_element_type=jnp.float32
    ).astype(jnp.bfloat16)
    sector_ids = jnp.arange(blocks, dtype=jnp.int32)
    assign = (targets[:, None, :] == sector_ids[None, :, None]).astype(jnp.bfloat16)
    row_slabs = halves.reshape(channels, blocks, bond_dim // blocks, col_width)
    received = lax.all_to_all(row_slabs, "sector", split_axis=1, concat_axis=1, tiled=True)
    summed = jnp.einsum(
        "ctq,cqrw->ctrw", assign, received, preferred_element_type=jnp.float32
    ).astype(jnp.bfloat16)
    returned = lax.all_to_all(summed, "sector", split_axis=1, concat_axis=1, tiled=True)
    gathered_cols = returned.reshape(channels, bond_dim, col_width)
    arrived = lax.all_to_all(gathered_cols, "shard", split_axis=1, concat_axis=2, tiled=True)
    local_rows = arrived.shape[1]
    phys_count = arrived.shape[2] // bond_dim
    stacked = arrived.reshape(channels, local_rows, phys_count, bond_dim)
    env_rows = lax.all_gather(right_environment[:, 0], "shard", axis=1, tiled=True)
    row_ids = jnp.arange(env_rows.shape[1], dtype=jnp.int32)
    keep_mask = (row_ids < right_live[group_index])[None, :, None] & own_right[None, None, :]
    env_live = jnp.where(keep_mask, env_rows, jnp.zeros_like(env_rows))
    result = jnp.einsum("crpk,cnk->rpn", stacked, env_live, preferred_element_type=jnp.float32)
    return result.reshape(1, local_rows, phys_count * bond_dim).astype(jnp.bfloat16)


def fits(mesh, shape):
    blocks, shards_n = mesh.shape["sector"], mesh.shape["shard"]
    bond = shape[1]
    local = shape[2] // shards_n
    if local % bond or bond % shards_n or not (is_pow2(blocks) and is_pow2(shards_n)) or shards_n != 8:
        return False
    col_parts = math.gcd(blocks, local // bond)
    return (bond // shards_n) % (blocks // col_parts * 16) == 0


def solution(mesh):
    def whole(*arrays):
        quick = fits(mesh, arrays[0].shape)
        mapped = jax.shard_map(
            fast if quick else shards,
            mesh=mesh,
            in_specs=(
                P("sector", None, "shard"),
                P(None, "sector", "shard", None),
                P(None, "sector", "shard", None),
                P(),
                P(),
            ),
            out_specs=P("sector", "shard", None),
            check_vma=False,
        )
        return mapped(*arrays)

    return whole
```

```python
import functools

import jax
import jax.numpy as jnp
from jax import lax
from jax.experimental import pallas as pl
from jax.experimental.pallas import tpu as pltpu
from jax.sharding import PartitionSpec as P


def is_pow2(n):
    return n & (n - 1) == 0


def exchange(x, axis, offset):
    size = lax.axis_size(axis)
    return lax.ppermute(x, axis, [(a, a ^ offset) for a in range(size)])


def gather_pieces(piece):
    pieces = []
    for m in range(0, lax.axis_size("shard"), 2):
        near = exchange(piece, "shard", m) if m else piece
        pieces += [near, exchange(near, "shard", 1)]
    return pieces


def live_mask(shape, rows_live, cols_live, row_start):
    row = lax.broadcasted_iota(jnp.int32, shape, 0) + row_start
    col = lax.broadcasted_iota(jnp.int32, shape, 1)
    return (row < rows_live) & (col < cols_live)


def mask_left(targets, sizes, channel, block):
    sector, shard = lax.axis_index("sector"), lax.axis_index("shard")
    rows = block.shape[0]
    keep = live_mask(block.shape, sizes[0, targets[channel, sector]], sizes[0, sector], shard * rows)
    return jnp.where(keep, block, 0).astype(block.dtype)


def prepare_kernel(targets, sizes, e_ref, f_ref, left, *rights):
    left[...] = mask_left(targets, sizes, 0, e_ref[0])
    for c, right in enumerate(rights):
        right[...] = f_ref[c]


def mask_right_kernel(targets, sizes, *refs, blocks, channel):
    sources, out, held = refs[:blocks], refs[-2], refs[-1]
    sector, shard = lax.axis_index("sector"), lax.axis_index("shard")
    target = targets[channel, sector]
    for k in range(blocks):
        @pl.when(target == sector ^ k)
        def _(k=k):
            held[...] = sources[k][...]
    live = sizes[1, target]
    keep = live_mask(held.shape, live, jnp.minimum(live, sizes[1, sector]), shard * held.shape[0])
    right = jnp.where(keep, held[...], 0).astype(held.dtype)
    if channel:
        out[0] = mask_left(targets, sizes, channel, refs[blocks][channel])
        out[1] = right
    else:
        out[...] = right


def prepare(targets, sizes, e_own, f_own):
    channels = f_own.shape[0]
    full, scalars = pl.BlockSpec(memory_space=pltpu.VMEM), pl.BlockSpec(memory_space=pltpu.SMEM)
    return pl.pallas_call(
        prepare_kernel,
        out_shape=[jax.ShapeDtypeStruct(e_own.shape[1:], jnp.bfloat16)] * (channels + 1),
        in_specs=[scalars, scalars, full, full],
        out_specs=[full] * (channels + 1),
        name="prepare",
    )(targets, sizes, e_own, f_own)


def masked_right(targets, sizes, f_parts, e_own, channel):
    rows, bond = e_own.shape[1:]
    full, scalars = pl.BlockSpec(memory_space=pltpu.VMEM), pl.BlockSpec(memory_space=pltpu.SMEM)
    extra = [e_own] * bool(channel)
    return pl.pallas_call(
        functools.partial(mask_right_kernel, blocks=len(f_parts), channel=channel),
        out_shape=jax.ShapeDtypeStruct((2, rows, bond) if channel else (rows, bond), jnp.bfloat16),
        in_specs=[scalars] * 2 + [full] * len(f_parts) + [full] * len(extra),
        out_specs=full,
        scratch_shapes=[pltpu.VMEM((rows, bond), jnp.bfloat16)],
        name="mask_right",
    )(targets, sizes, *f_parts, *extra)


def shard_chunks(shards_n):
    first = list(range(2, 2 + shards_n // 2))
    return first, [m for m in range(shards_n) if m not in first]


def products_kernel(*refs, shards_n, row_parts, col_parts, parts):
    y_refs = refs[-2 - row_parts * col_parts * parts:-2]
    pieces, psi_ref = refs[:-len(y_refs) - 3], refs[-len(y_refs) - 3]
    if len(pieces) == shards_n:
        pieces = [ref.at[n] for n in range(2) for ref in pieces]
    e_refs, f_refs = pieces[:shards_n], pieces[shards_n:]
    left_ref, right_ref = refs[-2:]
    rows, bond = e_refs[0].shape
    sub = rows // row_parts
    block = shards_n * sub
    sector, shard = lax.axis_index("sector"), lax.axis_index("shard")
    own_row, own_col = sector // col_parts, sector % col_parts
    for m in range(shards_n):
        right_ref[pl.ds(pl.multiple_of((shard ^ m) * rows, 16), rows), :] = f_refs[m][...]
    for n, m in enumerate(sum(shard_chunks(shards_n), [])):
        for h in range(row_parts):
            at = pl.multiple_of((own_row ^ h) * sub, 16)
            left_ref[h * block + n * sub:h * block + (n + 1) * sub, :] = e_refs[m][pl.ds(at, sub), :]
    for g in range(col_parts):
        at = pl.multiple_of((own_col ^ g) * bond, 128)
        half = jnp.dot(left_ref[...], psi_ref[:, pl.ds(at, bond)], preferred_element_type=jnp.float32)
        y = lax.dot_general(half.astype(jnp.bfloat16), right_ref[...], (((1,), (1,)), ((), ())),
                            preferred_element_type=jnp.float32).astype(jnp.bfloat16)
        size = block // parts
        for h in range(row_parts):
            for u in range(parts):
                start = h * block + u * size
                y_refs[(h * col_parts + g) * parts + u][...] = y[start:start + size]


def products(pieces, psi, shards_n, row_parts, col_parts, parts):
    rows, bond = pieces[0].shape[-2:]
    blocks = row_parts * col_parts
    full = pl.BlockSpec(memory_space=pltpu.VMEM)
    out = jax.ShapeDtypeStruct((shards_n * rows // row_parts // parts, bond), jnp.bfloat16)
    made = pl.pallas_call(
        functools.partial(products_kernel, shards_n=shards_n, row_parts=row_parts, col_parts=col_parts,
                          parts=parts),
        out_shape=[out] * (blocks * parts),
        in_specs=[full] * (len(pieces) + 1),
        out_specs=[full] * (blocks * parts),
        scratch_shapes=[pltpu.VMEM((bond, bond), jnp.bfloat16)] * 2,
        name="products",
    )(*pieces, psi)
    return [made[k * parts:(k + 1) * parts] for k in range(blocks)]


def sum_kernel(targets, *refs, blocks, own_n, steps):
    sources, outs = refs[:-own_n - blocks], refs[-own_n - blocks:-own_n - 1]
    own, acc = refs[-own_n - 1:-1], refs[-1]
    sub = own[0].shape[0]
    sector = lax.axis_index("sector")
    acc[...] = jnp.zeros_like(acc)
    for n, ref in enumerate(sources):
        j = targets[n // blocks, sector ^ (n % blocks)] ^ sector
        acc[j] = acc[j] + ref[...].astype(jnp.float32)
    for j in range(1, blocks):
        outs[j - 1][...] = acc[j].astype(jnp.bfloat16)
    per = own_n // steps
    for step in range(steps):
        @pl.when(pl.program_id(0) == step)
        def _(step=step):
            for n in range(per):
                own[step * per + n][...] = acc[0, n * sub:(n + 1) * sub].astype(jnp.bfloat16)


def destination_sums(targets, sources, starts, blocks, rows, own_n, steps):
    width = sources[0].shape[1]
    step, sub = rows // steps, rows // own_n
    specs = [pl.BlockSpec((step, width), lambda n, at=at // step: (n + at, 0)) for at in starts]
    return pl.pallas_call(
        functools.partial(sum_kernel, blocks=blocks, own_n=own_n, steps=steps),
        grid=(steps,),
        out_shape=[jax.ShapeDtypeStruct((rows, width), jnp.bfloat16)] * (blocks - 1)
        + [jax.ShapeDtypeStruct((sub, width), jnp.bfloat16)] * own_n,
        in_specs=[pl.BlockSpec(memory_space=pltpu.SMEM)] + specs,
        out_specs=[pl.BlockSpec((step, width), lambda n: (n, 0))] * (blocks - 1)
        + [pl.BlockSpec((sub, width), lambda n: (0, 0))] * own_n,
        scratch_shapes=[pltpu.VMEM((blocks, step, width), jnp.float32)],
        name="destination_sums",
    )(targets, *sources)


def fast(*arrays):
    return apply_blocks(*arrays)


def apply_blocks(wavefunction, left_environment, right_environment, targets, bond_sizes):
    sector = lax.axis_index("sector")
    shard = lax.axis_index("shard")
    blocks = lax.axis_size("sector")
    shards_n = lax.axis_size("shard")
    channels, _, rows, bond = left_environment.shape
    col_parts = wavefunction.shape[2] // bond
    row_parts = blocks // col_parts
    sub = rows // row_parts
    own_row, own_col = sector // col_parts, sector % col_parts
    psi = wavefunction[0]

    received = []
    e_own = left_environment[:, 0]
    left, *f_own = prepare(targets, bond_sizes, e_own, right_environment[:, 0])
    for c in range(channels):
        f_parts = [f_own[c]] + [exchange(f_own[c], "sector", k) for k in range(1, blocks)]
        right = masked_right(targets, bond_sizes, f_parts, e_own, c)
        if c:
            pieces = gather_pieces(right)
        else:
            pieces = gather_pieces(left) + gather_pieces(right)
        y = products(pieces, psi, shards_n, row_parts, col_parts, 2 if c + 1 == channels else 1)
        received.append([
            [exchange(part, "sector", k) if k else part for part in y[k]]
            for k in range(blocks)])

    placed = []
    for u, chunk in enumerate(shard_chunks(shards_n)):
        chunk_rows = len(chunk) * sub
        parts = [parts for channel in received for parts in channel]
        totals = destination_sums(
            targets, [p[u % len(p)] for p in parts], [0 if len(p) > 1 else u * chunk_rows for p in parts],
            blocks, chunk_rows, len(chunk), 2)
        for j in range(blocks):
            row_at = (own_row ^ (j // col_parts)) * sub
            col_at = (own_col ^ (j % col_parts)) * bond
            if j:
                total = exchange(totals[j - 1], "sector", j).reshape(len(chunk), sub, bond)
            for n, m in enumerate(chunk):
                part = total[n] if j else totals[blocks - 1 + n]
                part = exchange(part, "shard", m) if m else part
                placed.append((part, row_at, (shard ^ m) * col_parts * bond + col_at))
    out = jnp.zeros((rows, shards_n * col_parts * bond), jnp.bfloat16)
    for part, row_at, col_at in placed:
        out = lax.dynamic_update_slice(out, part, (row_at, col_at))
    return out[None]


def shards(wavefunction, left_environment, right_environment, targets, bond_sizes):
    group_index = lax.axis_index("sector")
    shard_index = lax.axis_index("shard")
    blocks = lax.axis_size("sector")
    channels = left_environment.shape[0]
    bond_dim = left_environment.shape[3]
    col_width = wavefunction.shape[2]
    positions = jnp.arange(bond_dim, dtype=jnp.int32)
    left_live = bond_sizes[0]
    right_live = bond_sizes[1]
    own_left = positions < left_live[group_index]
    own_right = positions < right_live[group_index]
    columns = shard_index * col_width + jnp.arange(col_width, dtype=jnp.int32)
    column_live = columns % bond_dim < right_live[group_index]
    psi_live = jnp.where(
        own_left[:, None] & column_live[None, :], wavefunction[0], jnp.zeros_like(wavefunction[0])
    )
    destination = targets[:, group_index]
    target_live = left_live[destination]
    env_rows = lax.all_gather(left_environment[:, 0], "shard", axis=1, tiled=True)
    row_ids = jnp.arange(env_rows.shape[1], dtype=jnp.int32)
    keep_mask = (row_ids[None, :, None] < target_live[:, None, None]) & own_left[None, None, :]
    env_live = jnp.where(keep_mask, env_rows, jnp.zeros_like(env_rows))
    halves = jnp.einsum(
        "crk,kw->crw", env_live, psi_live, preferred_element_type=jnp.float32
    ).astype(jnp.bfloat16)
    sector_ids = jnp.arange(blocks, dtype=jnp.int32)
    assign = (targets[:, None, :] == sector_ids[None, :, None]).astype(jnp.bfloat16)
    row_slabs = halves.reshape(channels, blocks, bond_dim // blocks, col_width)
    received = lax.all_to_all(row_slabs, "sector", split_axis=1, concat_axis=1, tiled=True)
    summed = jnp.einsum(
        "ctq,cqrw->ctrw", assign, received, preferred_element_type=jnp.float32
    ).astype(jnp.bfloat16)
    returned = lax.all_to_all(summed, "sector", split_axis=1, concat_axis=1, tiled=True)
    gathered_cols = returned.reshape(channels, bond_dim, col_width)
    arrived = lax.all_to_all(gathered_cols, "shard", split_axis=1, concat_axis=2, tiled=True)
    local_rows = arrived.shape[1]
    phys_count = arrived.shape[2] // bond_dim
    stacked = arrived.reshape(channels, local_rows, phys_count, bond_dim)
    env_rows = lax.all_gather(right_environment[:, 0], "shard", axis=1, tiled=True)
    row_ids = jnp.arange(env_rows.shape[1], dtype=jnp.int32)
    keep_mask = (row_ids < right_live[group_index])[None, :, None] & own_right[None, None, :]
    env_live = jnp.where(keep_mask, env_rows, jnp.zeros_like(env_rows))
    result = jnp.einsum("crpk,cnk->rpn", stacked, env_live, preferred_element_type=jnp.float32)
    return result.reshape(1, local_rows, phys_count * bond_dim).astype(jnp.bfloat16)


def fits(mesh, shape):
    blocks, shards_n = mesh.shape["sector"], mesh.shape["shard"]
    bond = shape[1]
    local = shape[2] // shards_n
    if local % bond or bond % shards_n or not (is_pow2(blocks) and is_pow2(shards_n)) or shards_n != 8:
        return False
    col_parts = local // bond
    return blocks % col_parts == 0 and is_pow2(col_parts) and (bond // shards_n) % (blocks // col_parts * 16) == 0


def solution(mesh):
    def whole(*arrays):
        quick = fits(mesh, arrays[0].shape)
        mapped = jax.shard_map(
            fast if quick else shards,
            mesh=mesh,
            in_specs=(
                P("sector", None, "shard"),
                P(None, "sector", "shard", None),
                P(None, "sector", "shard", None),
                P(),
                P(),
            ),
            out_specs=P("sector", "shard", None),
            check_vma=False,
        )
        return mapped(*arrays)

    return whole
```

```python
import functools

import jax
import jax.numpy as jnp
from jax import lax
from jax.experimental import pallas as pl
from jax.experimental.pallas import tpu as pltpu
from jax.sharding import PartitionSpec as P


def is_pow2(n):
    return n & (n - 1) == 0


def exchange(x, axis, offset):
    size = lax.axis_size(axis)
    return lax.ppermute(x, axis, [(a, a ^ offset) for a in range(size)])


def gather_pieces(piece):
    pieces = []
    for m in range(0, lax.axis_size("shard"), 2):
        near = exchange(piece, "shard", m) if m else piece
        pieces += [near, exchange(near, "shard", 1)]
    return pieces


def live_mask(shape, rows_live, cols_live, row_start):
    row = lax.broadcasted_iota(jnp.int32, shape, 0) + row_start
    col = lax.broadcasted_iota(jnp.int32, shape, 1)
    return (row < rows_live) & (col < cols_live)


def mask_left(targets, sizes, channel, block):
    sector, shard = lax.axis_index("sector"), lax.axis_index("shard")
    rows = block.shape[0]
    keep = live_mask(block.shape, sizes[0, targets[channel, sector]], sizes[0, sector], shard * rows)
    return jnp.where(keep, block, 0).astype(block.dtype)


def prepare_kernel(targets, sizes, e_ref, f_ref, left, *rights):
    left[...] = mask_left(targets, sizes, 0, e_ref[0])
    for c, right in enumerate(rights):
        right[...] = f_ref[c]


def mask_right_kernel(targets, sizes, *refs, blocks, channel):
    sources, out, held = refs[:blocks], refs[-2], refs[-1]
    sector, shard = lax.axis_index("sector"), lax.axis_index("shard")
    target = targets[channel, sector]
    for k in range(blocks):
        @pl.when(target == sector ^ k)
        def _(k=k):
            held[...] = sources[k][...]
    live = sizes[1, target]
    keep = live_mask(held.shape, live, jnp.minimum(live, sizes[1, sector]), shard * held.shape[0])
    right = jnp.where(keep, held[...], 0).astype(held.dtype)
    if channel:
        out[0] = mask_left(targets, sizes, channel, refs[blocks][channel])
        out[1] = right
    else:
        out[...] = right


def prepare(targets, sizes, e_own, f_own):
    channels = f_own.shape[0]
    full, scalars = pl.BlockSpec(memory_space=pltpu.VMEM), pl.BlockSpec(memory_space=pltpu.SMEM)
    return pl.pallas_call(
        prepare_kernel,
        out_shape=[jax.ShapeDtypeStruct(e_own.shape[1:], jnp.bfloat16)] * (channels + 1),
        in_specs=[scalars, scalars, full, full],
        out_specs=[full] * (channels + 1),
        name="prepare",
    )(targets, sizes, e_own, f_own)


def masked_right(targets, sizes, f_parts, e_own, channel):
    rows, bond = e_own.shape[1:]
    full, scalars = pl.BlockSpec(memory_space=pltpu.VMEM), pl.BlockSpec(memory_space=pltpu.SMEM)
    extra = [e_own] * bool(channel)
    return pl.pallas_call(
        functools.partial(mask_right_kernel, blocks=len(f_parts), channel=channel),
        out_shape=jax.ShapeDtypeStruct((2, rows, bond) if channel else (rows, bond), jnp.bfloat16),
        in_specs=[scalars] * 2 + [full] * len(f_parts) + [full] * len(extra),
        out_specs=full,
        scratch_shapes=[pltpu.VMEM((rows, bond), jnp.bfloat16)],
        name="mask_right",
    )(targets, sizes, *f_parts, *extra)


def shard_chunks(shards_n):
    first = [shards_n // 2, shards_n // 2 + 1, 2, 3]
    return first, [m for m in reversed(range(shards_n)) if m not in first]


def products_kernel(*refs, shards_n, row_parts, col_parts, parts):
    y_refs = refs[-2 - row_parts * col_parts * parts:-2]
    pieces, psi_ref = refs[:-len(y_refs) - 3], refs[-len(y_refs) - 3]
    if len(pieces) == shards_n:
        pieces = [ref.at[n] for n in range(2) for ref in pieces]
    e_refs, f_refs = pieces[:shards_n], pieces[shards_n:]
    left_ref, right_ref = refs[-2:]
    rows, bond = e_refs[0].shape
    sub = rows // row_parts
    block = shards_n * sub
    sector, shard = lax.axis_index("sector"), lax.axis_index("shard")
    own_row, own_col = sector // col_parts, sector % col_parts
    for m in range(shards_n):
        right_ref[pl.ds(pl.multiple_of((shard ^ m) * rows, 16), rows), :] = f_refs[m][...]
    for n, m in enumerate(sum(shard_chunks(shards_n), [])):
        for h in range(row_parts):
            at = pl.multiple_of((own_row ^ h) * sub, 16)
            left_ref[h * block + n * sub:h * block + (n + 1) * sub, :] = e_refs[m][pl.ds(at, sub), :]
    for g in range(col_parts):
        at = pl.multiple_of((own_col ^ g) * bond, 128)
        half = jnp.dot(left_ref[...], psi_ref[:, pl.ds(at, bond)], preferred_element_type=jnp.float32)
        y = lax.dot_general(half.astype(jnp.bfloat16), right_ref[...], (((1,), (1,)), ((), ())),
                            preferred_element_type=jnp.float32).astype(jnp.bfloat16)
        size = block // parts
        for h in range(row_parts):
            for u in range(parts):
                start = h * block + u * size
                y_refs[(h * col_parts + g) * parts + u][...] = y[start:start + size]


def products(pieces, psi, shards_n, row_parts, col_parts, parts):
    rows, bond = pieces[0].shape[-2:]
    blocks = row_parts * col_parts
    full = pl.BlockSpec(memory_space=pltpu.VMEM)
    out = jax.ShapeDtypeStruct((shards_n * rows // row_parts // parts, bond), jnp.bfloat16)
    made = pl.pallas_call(
        functools.partial(products_kernel, shards_n=shards_n, row_parts=row_parts, col_parts=col_parts,
                          parts=parts),
        out_shape=[out] * (blocks * parts),
        in_specs=[full] * (len(pieces) + 1),
        out_specs=[full] * (blocks * parts),
        scratch_shapes=[pltpu.VMEM((bond, bond), jnp.bfloat16)] * 2,
        name="products",
    )(*pieces, psi)
    return [made[k * parts:(k + 1) * parts] for k in range(blocks)]


def sum_kernel(targets, *refs, blocks, own_n, steps):
    sources, outs = refs[:-own_n - blocks], refs[-own_n - blocks:-own_n - 1]
    own, acc = refs[-own_n - 1:-1], refs[-1]
    sub = own[0].shape[0]
    sector = lax.axis_index("sector")
    acc[...] = jnp.zeros_like(acc)
    for n, ref in enumerate(sources):
        j = targets[n // blocks, sector ^ (n % blocks)] ^ sector
        acc[j] = acc[j] + ref[...].astype(jnp.float32)
    for j in range(1, blocks):
        outs[j - 1][...] = acc[j].astype(jnp.bfloat16)
    per = own_n // steps
    for step in range(steps):
        @pl.when(pl.program_id(0) == step)
        def _(step=step):
            for n in range(per):
                own[step * per + n][...] = acc[0, n * sub:(n + 1) * sub].astype(jnp.bfloat16)


def destination_sums(targets, sources, starts, blocks, rows, own_n, steps):
    width = sources[0].shape[1]
    step, sub = rows // steps, rows // own_n
    specs = [pl.BlockSpec((step, width), lambda n, at=at // step: (n + at, 0)) for at in starts]
    return pl.pallas_call(
        functools.partial(sum_kernel, blocks=blocks, own_n=own_n, steps=steps),
        grid=(steps,),
        out_shape=[jax.ShapeDtypeStruct((rows, width), jnp.bfloat16)] * (blocks - 1)
        + [jax.ShapeDtypeStruct((sub, width), jnp.bfloat16)] * own_n,
        in_specs=[pl.BlockSpec(memory_space=pltpu.SMEM)] + specs,
        out_specs=[pl.BlockSpec((step, width), lambda n: (n, 0))] * (blocks - 1)
        + [pl.BlockSpec((sub, width), lambda n: (0, 0))] * own_n,
        scratch_shapes=[pltpu.VMEM((blocks, step, width), jnp.float32)],
        name="destination_sums",
    )(targets, *sources)


def fast(*arrays):
    return apply_blocks(*arrays)


def apply_blocks(wavefunction, left_environment, right_environment, targets, bond_sizes):
    sector = lax.axis_index("sector")
    shard = lax.axis_index("shard")
    blocks = lax.axis_size("sector")
    shards_n = lax.axis_size("shard")
    channels, _, rows, bond = left_environment.shape
    col_parts = wavefunction.shape[2] // bond
    row_parts = blocks // col_parts
    sub = rows // row_parts
    own_row, own_col = sector // col_parts, sector % col_parts
    psi = wavefunction[0]

    received = []
    e_own = left_environment[:, 0]
    left, *f_own = prepare(targets, bond_sizes, e_own, right_environment[:, 0])
    for c in range(channels):
        f_parts = [f_own[c]] + [exchange(f_own[c], "sector", k) for k in range(1, blocks)]
        right = masked_right(targets, bond_sizes, f_parts, e_own, c)
        if c:
            pieces = gather_pieces(right)
        else:
            pieces = gather_pieces(left) + gather_pieces(right)
        y = products(pieces, psi, shards_n, row_parts, col_parts, 2 if c + 1 == channels else 1)
        received.append([
            [exchange(part, "sector", k) if k else part for part in y[k]]
            for k in range(blocks)])

    placed = []
    for u, chunk in enumerate(shard_chunks(shards_n)):
        chunk_rows = len(chunk) * sub
        parts = [parts for channel in received for parts in channel]
        totals = destination_sums(
            targets, [p[u % len(p)] for p in parts], [0 if len(p) > 1 else u * chunk_rows for p in parts],
            blocks, chunk_rows, len(chunk), 1 + len(chunk) % 2 * (len(chunk) - 1) if len(chunk) % 2 else 2)
        for j in range(blocks):
            row_at = (own_row ^ (j // col_parts)) * sub
            col_at = (own_col ^ (j % col_parts)) * bond
            if j:
                total = exchange(totals[j - 1], "sector", j).reshape(len(chunk), sub, bond)
            for n, m in enumerate(chunk):
                part = total[n] if j else totals[blocks - 1 + n]
                part = exchange(part, "shard", m) if m else part
                placed.append((part, row_at, (shard ^ m) * col_parts * bond + col_at))
    out = jnp.zeros((rows, shards_n * col_parts * bond), jnp.bfloat16)
    for part, row_at, col_at in placed:
        out = lax.dynamic_update_slice(out, part, (row_at, col_at))
    return out[None]


def shards(wavefunction, left_environment, right_environment, targets, bond_sizes):
    group_index = lax.axis_index("sector")
    shard_index = lax.axis_index("shard")
    blocks = lax.axis_size("sector")
    channels = left_environment.shape[0]
    bond_dim = left_environment.shape[3]
    col_width = wavefunction.shape[2]
    positions = jnp.arange(bond_dim, dtype=jnp.int32)
    left_live = bond_sizes[0]
    right_live = bond_sizes[1]
    own_left = positions < left_live[group_index]
    own_right = positions < right_live[group_index]
    columns = shard_index * col_width + jnp.arange(col_width, dtype=jnp.int32)
    column_live = columns % bond_dim < right_live[group_index]
    psi_live = jnp.where(
        own_left[:, None] & column_live[None, :], wavefunction[0], jnp.zeros_like(wavefunction[0])
    )
    destination = targets[:, group_index]
    target_live = left_live[destination]
    env_rows = lax.all_gather(left_environment[:, 0], "shard", axis=1, tiled=True)
    row_ids = jnp.arange(env_rows.shape[1], dtype=jnp.int32)
    keep_mask = (row_ids[None, :, None] < target_live[:, None, None]) & own_left[None, None, :]
    env_live = jnp.where(keep_mask, env_rows, jnp.zeros_like(env_rows))
    halves = jnp.einsum(
        "crk,kw->crw", env_live, psi_live, preferred_element_type=jnp.float32
    ).astype(jnp.bfloat16)
    sector_ids = jnp.arange(blocks, dtype=jnp.int32)
    assign = (targets[:, None, :] == sector_ids[None, :, None]).astype(jnp.bfloat16)
    row_slabs = halves.reshape(channels, blocks, bond_dim // blocks, col_width)
    received = lax.all_to_all(row_slabs, "sector", split_axis=1, concat_axis=1, tiled=True)
    summed = jnp.einsum(
        "ctq,cqrw->ctrw", assign, received, preferred_element_type=jnp.float32
    ).astype(jnp.bfloat16)
    returned = lax.all_to_all(summed, "sector", split_axis=1, concat_axis=1, tiled=True)
    gathered_cols = returned.reshape(channels, bond_dim, col_width)
    arrived = lax.all_to_all(gathered_cols, "shard", split_axis=1, concat_axis=2, tiled=True)
    local_rows = arrived.shape[1]
    phys_count = arrived.shape[2] // bond_dim
    stacked = arrived.reshape(channels, local_rows, phys_count, bond_dim)
    env_rows = lax.all_gather(right_environment[:, 0], "shard", axis=1, tiled=True)
    row_ids = jnp.arange(env_rows.shape[1], dtype=jnp.int32)
    keep_mask = (row_ids < right_live[group_index])[None, :, None] & own_right[None, None, :]
    env_live = jnp.where(keep_mask, env_rows, jnp.zeros_like(env_rows))
    result = jnp.einsum("crpk,cnk->rpn", stacked, env_live, preferred_element_type=jnp.float32)
    return result.reshape(1, local_rows, phys_count * bond_dim).astype(jnp.bfloat16)


def fits(mesh, shape):
    blocks, shards_n = mesh.shape["sector"], mesh.shape["shard"]
    bond = shape[1]
    local = shape[2] // shards_n
    if local % bond or bond % shards_n or not (is_pow2(blocks) and is_pow2(shards_n)) or shards_n != 8 or blocks != 4:
        return False
    col_parts = local // bond
    return blocks % col_parts == 0 and is_pow2(col_parts) and (bond // shards_n) % (blocks // col_parts * 16) == 0


def solution(mesh):
    def whole(*arrays):
        quick = fits(mesh, arrays[0].shape)
        mapped = jax.shard_map(
            fast if quick else shards,
            mesh=mesh,
            in_specs=(
                P("sector", None, "shard"),
                P(None, "sector", "shard", None),
                P(None, "sector", "shard", None),
                P(),
                P(),
            ),
            out_specs=P("sector", "shard", None),
            check_vma=False,
        )
        return mapped(*arrays)

    return whole
```

```python
import functools

import jax
import jax.numpy as jnp
from jax import lax
from jax.experimental import pallas as pl
from jax.experimental.pallas import tpu as pltpu
from jax.sharding import PartitionSpec as P


def is_pow2(n):
    return n & (n - 1) == 0


def exchange(x, axis, offset):
    size = lax.axis_size(axis)
    return lax.ppermute(x, axis, [(a, a ^ offset) for a in range(size)])


def gather_pieces(piece):
    pieces = []
    for m in range(0, lax.axis_size("shard"), 2):
        near = exchange(piece, "shard", m) if m else piece
        pieces += [near, exchange(near, "shard", 1)]
    return pieces


def live_mask(shape, rows_live, cols_live, row_start):
    row = lax.broadcasted_iota(jnp.int32, shape, 0) + row_start
    col = lax.broadcasted_iota(jnp.int32, shape, 1)
    return (row < rows_live) & (col < cols_live)


def mask_left(targets, sizes, channel, block):
    sector, shard = lax.axis_index("sector"), lax.axis_index("shard")
    rows = block.shape[0]
    keep = live_mask(block.shape, sizes[0, targets[channel, sector]], sizes[0, sector], shard * rows)
    return jnp.where(keep, block, 0).astype(block.dtype)


def prepare_kernel(targets, sizes, e_ref, f_ref, left, *rights):
    left[...] = mask_left(targets, sizes, 0, e_ref[0])
    for c, right in enumerate(rights):
        right[...] = f_ref[c]


def mask_right_kernel(targets, sizes, *refs, blocks, channel):
    sources, out, held = refs[:blocks], refs[-2], refs[-1]
    sector, shard = lax.axis_index("sector"), lax.axis_index("shard")
    target = targets[channel, sector]
    for k in range(blocks):
        @pl.when(target == sector ^ k)
        def _(k=k):
            held[...] = sources[k][...]
    live = sizes[1, target]
    keep = live_mask(held.shape, live, jnp.minimum(live, sizes[1, sector]), shard * held.shape[0])
    right = jnp.where(keep, held[...], 0).astype(held.dtype)
    if channel:
        out[0] = mask_left(targets, sizes, channel, refs[blocks][channel])
        out[1] = right
    else:
        out[...] = right


def prepare(targets, sizes, e_own, f_own):
    channels = f_own.shape[0]
    full, scalars = pl.BlockSpec(memory_space=pltpu.VMEM), pl.BlockSpec(memory_space=pltpu.SMEM)
    return pl.pallas_call(
        prepare_kernel,
        out_shape=[jax.ShapeDtypeStruct(e_own.shape[1:], jnp.bfloat16)] * (channels + 1),
        in_specs=[scalars, scalars, full, full],
        out_specs=[full] * (channels + 1),
        name="prepare",
    )(targets, sizes, e_own, f_own)


def masked_right(targets, sizes, f_parts, e_own, channel):
    rows, bond = e_own.shape[1:]
    full, scalars = pl.BlockSpec(memory_space=pltpu.VMEM), pl.BlockSpec(memory_space=pltpu.SMEM)
    extra = [e_own] * bool(channel)
    return pl.pallas_call(
        functools.partial(mask_right_kernel, blocks=len(f_parts), channel=channel),
        out_shape=jax.ShapeDtypeStruct((2, rows, bond) if channel else (rows, bond), jnp.bfloat16),
        in_specs=[scalars] * 2 + [full] * len(f_parts) + [full] * len(extra),
        out_specs=full,
        scratch_shapes=[pltpu.VMEM((rows, bond), jnp.bfloat16)],
        name="mask_right",
    )(targets, sizes, *f_parts, *extra)


def shard_chunks(shards_n):
    first = [shards_n // 2, shards_n // 2 + 1, 2, 3]
    return first, [m for m in reversed(range(shards_n)) if m not in first]


def products_kernel(*refs, shards_n, row_parts, col_parts, parts):
    y_refs = refs[-2 - row_parts * col_parts * parts:-2]
    pieces, psi_ref = refs[:-len(y_refs) - 3], refs[-len(y_refs) - 3]
    if len(pieces) == shards_n:
        pieces = [ref.at[n] for n in range(2) for ref in pieces]
    e_refs, f_refs = pieces[:shards_n], pieces[shards_n:]
    left_ref, right_ref = refs[-2:]
    rows, bond = e_refs[0].shape
    sub = rows // row_parts
    block = shards_n * sub
    sector, shard = lax.axis_index("sector"), lax.axis_index("shard")
    own_row, own_col = sector // col_parts, sector % col_parts
    for m in range(shards_n):
        right_ref[pl.ds(pl.multiple_of((shard ^ m) * rows, 16), rows), :] = f_refs[m][...]
    for n, m in enumerate(sum(shard_chunks(shards_n), [])):
        for h in range(row_parts):
            at = pl.multiple_of((own_row ^ h) * sub, 16)
            left_ref[h * block + n * sub:h * block + (n + 1) * sub, :] = e_refs[m][pl.ds(at, sub), :]
    for g in range(col_parts):
        at = pl.multiple_of((own_col ^ g) * bond, 128)
        half = jnp.dot(left_ref[...], psi_ref[:, pl.ds(at, bond)], preferred_element_type=jnp.float32)
        y = lax.dot_general(half.astype(jnp.bfloat16), right_ref[...], (((1,), (1,)), ((), ())),
                            preferred_element_type=jnp.float32).astype(jnp.bfloat16)
        size = block // parts
        for h in range(row_parts):
            for u in range(parts):
                start = h * block + u * size
                y_refs[(h * col_parts + g) * parts + u][...] = y[start:start + size]


def products(pieces, psi, shards_n, row_parts, col_parts, parts):
    rows, bond = pieces[0].shape[-2:]
    blocks = row_parts * col_parts
    full = pl.BlockSpec(memory_space=pltpu.VMEM)
    out = jax.ShapeDtypeStruct((shards_n * rows // row_parts // parts, bond), jnp.bfloat16)
    made = pl.pallas_call(
        functools.partial(products_kernel, shards_n=shards_n, row_parts=row_parts, col_parts=col_parts,
                          parts=parts),
        out_shape=[out] * (blocks * parts),
        in_specs=[full] * (len(pieces) + 1),
        out_specs=[full] * (blocks * parts),
        scratch_shapes=[pltpu.VMEM((bond, bond), jnp.bfloat16)] * 2,
        name="products",
    )(*pieces, psi)
    return [made[k * parts:(k + 1) * parts] for k in range(blocks)]


def stack_kernel(*refs):
    for n, ref in enumerate(refs[:-1]):
        refs[-1][n] = ref[...]


def stacked(sources):
    full = pl.BlockSpec(memory_space=pltpu.VMEM)
    return pl.pallas_call(
        stack_kernel,
        out_shape=jax.ShapeDtypeStruct((len(sources), *sources[0].shape), jnp.bfloat16),
        in_specs=[full] * len(sources),
        out_specs=full,
        name="stacked",
    )(*sources)


def sum_kernel(targets, *refs, blocks, own_n, steps):
    sources, outs = refs[1:-own_n - blocks], refs[-own_n - blocks:-own_n - 1]
    sources = [refs[0].at[n] for n in range(refs[0].shape[0])] + list(sources)
    own, acc = refs[-own_n - 1:-1], refs[-1]
    sub = own[0].shape[0]
    sector = lax.axis_index("sector")
    acc[...] = jnp.zeros_like(acc)
    for n, ref in enumerate(sources):
        j = targets[n // blocks, sector ^ (n % blocks)] ^ sector
        acc[j] = acc[j] + ref[...].astype(jnp.float32)
    for j in range(1, blocks):
        outs[j - 1][...] = acc[j].astype(jnp.bfloat16)
    per = own_n // steps
    for step in range(steps):
        @pl.when(pl.program_id(0) == step)
        def _(step=step):
            for n in range(per):
                own[step * per + n][...] = acc[0, n * sub:(n + 1) * sub].astype(jnp.bfloat16)


def destination_sums(targets, early, sources, start, blocks, rows, own_n, steps):
    width = sources[0].shape[1]
    step, sub = rows // steps, rows // own_n
    specs = [pl.BlockSpec((early.shape[0], step, width), lambda n: (0, n + start // step, 0))]
    specs += [pl.BlockSpec((step, width), lambda n: (n, 0))] * len(sources)
    return pl.pallas_call(
        functools.partial(sum_kernel, blocks=blocks, own_n=own_n, steps=steps),
        grid=(steps,),
        out_shape=[jax.ShapeDtypeStruct((rows, width), jnp.bfloat16)] * (blocks - 1)
        + [jax.ShapeDtypeStruct((sub, width), jnp.bfloat16)] * own_n,
        in_specs=[pl.BlockSpec(memory_space=pltpu.SMEM)] + specs,
        out_specs=[pl.BlockSpec((step, width), lambda n: (n, 0))] * (blocks - 1)
        + [pl.BlockSpec((sub, width), lambda n: (0, 0))] * own_n,
        scratch_shapes=[pltpu.VMEM((blocks, step, width), jnp.float32)],
        name="destination_sums",
    )(targets, early, *sources)


def fast(*arrays):
    return apply_blocks(*arrays)


def apply_blocks(wavefunction, left_environment, right_environment, targets, bond_sizes):
    sector = lax.axis_index("sector")
    shard = lax.axis_index("shard")
    blocks = lax.axis_size("sector")
    shards_n = lax.axis_size("shard")
    channels, _, rows, bond = left_environment.shape
    col_parts = wavefunction.shape[2] // bond
    row_parts = blocks // col_parts
    sub = rows // row_parts
    own_row, own_col = sector // col_parts, sector % col_parts
    psi = wavefunction[0]

    received = []
    e_own = left_environment[:, 0]
    left, *f_own = prepare(targets, bond_sizes, e_own, right_environment[:, 0])
    for c in range(channels):
        f_parts = [f_own[c]] + [exchange(f_own[c], "sector", k) for k in range(1, blocks)]
        right = masked_right(targets, bond_sizes, f_parts, e_own, c)
        if c:
            pieces = gather_pieces(right)
        else:
            pieces = gather_pieces(left) + gather_pieces(right)
        y = products(pieces, psi, shards_n, row_parts, col_parts, 2 if c + 1 == channels else 1)
        received.append([
            [exchange(part, "sector", k) if k else part for part in y[k]]
            for k in range(blocks)])

    placed = []
    early = stacked([part for channel in received[:-1] for parts in channel for part in parts])
    for u, chunk in enumerate(shard_chunks(shards_n)):
        chunk_rows = len(chunk) * sub
        totals = destination_sums(
            targets, early, [parts[u] for parts in received[-1]], u * chunk_rows, blocks, chunk_rows, len(chunk), 2)
        for j in range(blocks):
            row_at = (own_row ^ (j // col_parts)) * sub
            col_at = (own_col ^ (j % col_parts)) * bond
            if j:
                total = exchange(totals[j - 1], "sector", j).reshape(len(chunk), sub, bond)
            for n, m in enumerate(chunk):
                part = total[n] if j else totals[blocks - 1 + n]
                part = exchange(part, "shard", m) if m else part
                placed.append((part, row_at, (shard ^ m) * col_parts * bond + col_at))
    out = jnp.zeros((rows, shards_n * col_parts * bond), jnp.bfloat16)
    for part, row_at, col_at in placed:
        out = lax.dynamic_update_slice(out, part, (row_at, col_at))
    return out[None]


def shards(wavefunction, left_environment, right_environment, targets, bond_sizes):
    group_index = lax.axis_index("sector")
    shard_index = lax.axis_index("shard")
    blocks = lax.axis_size("sector")
    channels = left_environment.shape[0]
    bond_dim = left_environment.shape[3]
    col_width = wavefunction.shape[2]
    positions = jnp.arange(bond_dim, dtype=jnp.int32)
    left_live = bond_sizes[0]
    right_live = bond_sizes[1]
    own_left = positions < left_live[group_index]
    own_right = positions < right_live[group_index]
    columns = shard_index * col_width + jnp.arange(col_width, dtype=jnp.int32)
    column_live = columns % bond_dim < right_live[group_index]
    psi_live = jnp.where(
        own_left[:, None] & column_live[None, :], wavefunction[0], jnp.zeros_like(wavefunction[0])
    )
    destination = targets[:, group_index]
    target_live = left_live[destination]
    env_rows = lax.all_gather(left_environment[:, 0], "shard", axis=1, tiled=True)
    row_ids = jnp.arange(env_rows.shape[1], dtype=jnp.int32)
    keep_mask = (row_ids[None, :, None] < target_live[:, None, None]) & own_left[None, None, :]
    env_live = jnp.where(keep_mask, env_rows, jnp.zeros_like(env_rows))
    halves = jnp.einsum(
        "crk,kw->crw", env_live, psi_live, preferred_element_type=jnp.float32
    ).astype(jnp.bfloat16)
    sector_ids = jnp.arange(blocks, dtype=jnp.int32)
    assign = (targets[:, None, :] == sector_ids[None, :, None]).astype(jnp.bfloat16)
    row_slabs = halves.reshape(channels, blocks, bond_dim // blocks, col_width)
    received = lax.all_to_all(row_slabs, "sector", split_axis=1, concat_axis=1, tiled=True)
    summed = jnp.einsum(
        "ctq,cqrw->ctrw", assign, received, preferred_element_type=jnp.float32
    ).astype(jnp.bfloat16)
    returned = lax.all_to_all(summed, "sector", split_axis=1, concat_axis=1, tiled=True)
    gathered_cols = returned.reshape(channels, bond_dim, col_width)
    arrived = lax.all_to_all(gathered_cols, "shard", split_axis=1, concat_axis=2, tiled=True)
    local_rows = arrived.shape[1]
    phys_count = arrived.shape[2] // bond_dim
    stacked = arrived.reshape(channels, local_rows, phys_count, bond_dim)
    env_rows = lax.all_gather(right_environment[:, 0], "shard", axis=1, tiled=True)
    row_ids = jnp.arange(env_rows.shape[1], dtype=jnp.int32)
    keep_mask = (row_ids < right_live[group_index])[None, :, None] & own_right[None, None, :]
    env_live = jnp.where(keep_mask, env_rows, jnp.zeros_like(env_rows))
    result = jnp.einsum("crpk,cnk->rpn", stacked, env_live, preferred_element_type=jnp.float32)
    return result.reshape(1, local_rows, phys_count * bond_dim).astype(jnp.bfloat16)


def fits(mesh, shape):
    blocks, shards_n = mesh.shape["sector"], mesh.shape["shard"]
    bond = shape[1]
    local = shape[2] // shards_n
    if local % bond or bond % shards_n or not (is_pow2(blocks) and is_pow2(shards_n)) or shards_n != 8 or blocks != 4:
        return False
    col_parts = local // bond
    return blocks % col_parts == 0 and is_pow2(col_parts) and (bond // shards_n) % (blocks // col_parts * 16) == 0


def solution(mesh):
    def whole(*arrays):
        quick = fits(mesh, arrays[0].shape)
        mapped = jax.shard_map(
            fast if quick else shards,
            mesh=mesh,
            in_specs=(
                P("sector", None, "shard"),
                P(None, "sector", "shard", None),
                P(None, "sector", "shard", None),
                P(),
                P(),
            ),
            out_specs=P("sector", "shard", None),
            check_vma=False,
        )
        return mapped(*arrays)

    return whole
```
